256 devices in a mesh: row: 8 (over z), col: 16 (over y, x), pan: 2 (over core).
Axes of the slice: x: 4, y: 4, z: 8, core: 2. Of those that a mesh axis runs over, the one named last changes fastest.
Arguments:
- plan_values: bfloat16 [8192, 128, 256], P('row', 'col', 'pan'), may hold values from 0.099609375 to 1
- plan_blocks: int32 [8, 128], P('row', 'col'), may hold values from 0 to 127, as said below
- first_values: bfloat16 [32, 3, 256, 256], P('row'), may hold values from -0.21875 to 0.21875
- first_blocks: int32 [32, 3], P('row'), may hold values from 0 to 3, as said below
- second_values: bfloat16 [128, 6, 256, 256], P('col', None, None, 'pan'), may hold values from -0.15625 to 0.15625
- second_blocks: int32 [128, 6], P('col'), may hold values from 0 to 7, as said below
- weight_first: float32 [8192], P('row'), may hold values from 0.5 to 2
- weight_second: float32 [128, 256], P('col', 'pan'), may hold values from 0.5 to 2
- offset_first: float32 [8192], P('row'), may hold values from -3 to 3
- offset_second: float32 [128, 256], P('col', 'pan'), may hold values from -3 to 3
Outputs:
- new_plan: bfloat16 [8192, 128, 256], P('row', 'col', 'pan')
- scale_first: float32 [8192], P('row')
- scale_second: float32 [128, 256], P('col', 'pan')
The draws below stay inside these ranges and needn't reach their ends.
Inputs may be any that keep to these rules, and one draw needn't show every extreme that they name: `plan_blocks`: each entry is a slice-B block number; its column panel is the entry // 8. Within the 8 slots of one index of col (aligned groups of the second dimension) no column panel is named more than 2 times, and in every row panel one column panel is named exactly 2 times by every such group. `first_blocks`: block numbers within the row panel of the slice-A block; the 3 entries of a row are distinct. `second_blocks`: block numbers within the column panel of the slice-B block; the 6 entries of a row are distinct.
All inputs are finite; a program needn't handle non-finite values.
Results may differ from the reference program's by a relative error of at most 0.0087.
Values may be sent and summed in bfloat16 or wider, within the bound.
No kernel may reach another device: no remote copies, remote signals or barrier semaphores. Data moves between devices by JAX's collectives and lax.ppermute only.
A program may use at most 128 MiB of HBM per device.

```python
import math
import jax
import jax.numpy as jnp

BLOCK = 256
PANEL_BLOCKS = 4
COL_BLOCKS = 8
FIRST_NEAR = 3
SECOND_NEAR = 6
PLAN_SLOTS = 8
CAP = 2
PANELS = 8
COL_PANELS = 16
PANEL_ROWS = 1024
ROW_BLOCKS_A = 32
ROWS_A = 8192
BLOCKS_B = 128
PLAN_WIDTH = 128


def draw_plan_blocks(key, part):
    folded = jax.random.fold_in(key, 7)
    subkeys = jax.random.split(folded, 4)
    hot_panel = jax.random.randint(subkeys[0], (PANELS, 1, 1), 0, COL_PANELS)
    spare_panels = COL_PANELS - 1
    scores = jax.random.randint(subkeys[1], (PANELS, COL_PANELS, spare_panels), 0, 1 << 20) * spare_panels + jnp.arange(spare_panels, dtype=jnp.int32)[None, None, :]
    ordering = jnp.argsort(scores, axis=-1).astype(jnp.int32)
    spare_slots = PLAN_SLOTS - CAP
    chosen = ordering[:, :, jnp.arange(spare_slots, dtype=jnp.int32) % spare_panels]
    far_panel = (hot_panel + 1 + chosen) % COL_PANELS
    near_panel = jnp.broadcast_to(hot_panel, (PANELS, COL_PANELS, CAP))
    panels_drawn = jnp.concatenate([near_panel, far_panel], axis=-1)
    shuffle_scores = jax.random.randint(subkeys[2], (PANELS, COL_PANELS, PLAN_SLOTS), 0, 1 << 20) * PLAN_SLOTS + jnp.arange(PLAN_SLOTS, dtype=jnp.int32)[None, None, :]
    shuffle = jnp.argsort(shuffle_scores, axis=-1).astype(jnp.int32)
    panels_drawn = jnp.take_along_axis(panels_drawn, shuffle, axis=-1)
    inside = jax.random.randint(subkeys[3], (PANELS, COL_PANELS, PLAN_SLOTS), 0, COL_BLOCKS)
    return (panels_drawn * COL_BLOCKS + inside).reshape(PANELS, COL_PANELS * PLAN_SLOTS).astype(jnp.int32)


def distinct_rows(key, row_count, choices_count, taken):
    scores = jax.random.randint(key, (row_count, choices_count), 0, 1 << 20) * choices_count + jnp.arange(choices_count, dtype=jnp.int32)[None, :]
    ordering = jnp.argsort(scores, axis=-1).astype(jnp.int32)
    return ordering[:, :taken].astype(jnp.int32)


def draw_first_blocks(key, part):
    return distinct_rows(jax.random.fold_in(key, 11), ROW_BLOCKS_A, PANEL_BLOCKS, FIRST_NEAR)


def draw_second_blocks(key, part):
    return distinct_rows(jax.random.fold_in(key, 13), BLOCKS_B, COL_BLOCKS, SECOND_NEAR)


def block_scale(key, extent, cuts, smallest, largest):
    level, own = 1.0, jax.random.fold_in(key, 6)
    for axis_at, parts in cuts:
        steps = jnp.exp(jax.random.uniform(jax.random.fold_in(own, axis_at), (parts,), jnp.float32, smallest / len(cuts), largest / len(cuts)))
        level = level * jnp.repeat(steps, extent[axis_at] // parts).reshape([-1 if axis == axis_at else 1 for axis in range(len(extent))])
    return level


def noise(rng, shape, scale, most, cuts=(), kind=jnp.bfloat16):
    result = scale * jax.random.normal(rng, shape, jnp.float32)
    if cuts:
        result = result * block_scale(rng, shape, cuts, -0.22, 0.18)
    return jnp.clip(result, -most, most).astype(kind)


def setup_inputs(seed: int = 0) -> dict:
    key_list = jax.random.split(jax.random.key(seed), 11)
    return {
        "plan_values": jnp.clip(jnp.exp(math.log(1.0) - 2.306499 * jax.random.uniform(key_list[0], (ROWS_A, PLAN_WIDTH, BLOCK), jnp.float32) ** block_scale(key_list[0], (ROWS_A, PLAN_WIDTH, BLOCK), ((0, 8), (1, 16), (2, 2)), -0.2, 0.2)), 0.099609375, 1.0).astype(jnp.bfloat16),
        "plan_blocks": draw_plan_blocks(jax.random.fold_in(key_list[10], 71), 0),
        "first_values": noise(key_list[2], (ROW_BLOCKS_A, FIRST_NEAR, BLOCK, BLOCK), (BLOCK * FIRST_NEAR) ** -0.5, 0.21875, ((0, 8),)),
        "first_blocks": draw_first_blocks(jax.random.fold_in(key_list[10], 71), 0),
        "second_values": noise(key_list[4], (BLOCKS_B, SECOND_NEAR, BLOCK, BLOCK), (BLOCK * SECOND_NEAR) ** -0.5, 0.15625, ((0, 16), (3, 2))),
        "second_blocks": draw_second_blocks(jax.random.fold_in(key_list[10], 71), 0),
        "weight_first": jnp.clip(jnp.exp(math.log(2.0) - 1.3862944 * jax.random.uniform(key_list[6], (ROWS_A,), jnp.float32) ** block_scale(key_list[6], (ROWS_A,), ((0, 8),), -0.2, 0.2)), 0.5, 2.0),
        "weight_second": jnp.clip(jnp.exp(math.log(2.0) - 1.3862944 * jax.random.uniform(key_list[7], (BLOCKS_B, BLOCK), jnp.float32) ** block_scale(key_list[7], (BLOCKS_B, BLOCK), ((0, 16), (1, 2)), -0.2, 0.2)), 0.5, 2.0),
        "offset_first": noise(key_list[8], (ROWS_A,), 0.5, 3.0, ((0, 8),), jnp.float32),
        "offset_second": noise(key_list[9], (BLOCKS_B, BLOCK), 0.5, 3.0, ((0, 16), (1, 2)), jnp.float32),
    }


def reference(plan_values, plan_blocks, first_values, first_blocks, second_values, second_blocks, weight_first, weight_second, offset_first, offset_second):
    panel_rows = PANEL_ROWS
    plan_width = PLAN_WIDTH * BLOCK
    panel_base = (jnp.arange(BLOCKS_B, dtype=jnp.int32) // COL_BLOCKS) * COL_BLOCKS
    kept_blocks = []
    row_scales = []
    colsum = jnp.zeros((BLOCKS_B, BLOCK), jnp.float32)
    counts = jnp.zeros((BLOCKS_B,), jnp.float32)
    for panel_index in range(PANELS):
        row_start = panel_index * panel_rows
        row_tiles = plan_values[row_start:row_start + panel_rows].reshape(PANEL_BLOCKS, BLOCK, plan_width)
        near_list = first_blocks[panel_index * PANEL_BLOCKS:(panel_index + 1) * PANEL_BLOCKS].astype(jnp.int32)
        coefficients = first_values[panel_index * PANEL_BLOCKS:(panel_index + 1) * PANEL_BLOCKS]
        running = jnp.zeros((PANEL_BLOCKS, BLOCK, plan_width), jnp.float32)
        for neighbor in range(FIRST_NEAR):
            picked = row_tiles[near_list[:, neighbor]].astype(jnp.float32)
            running = running + jnp.einsum("iab,ibn->ian", coefficients[:, neighbor].astype(jnp.float32), picked)
        product = running.astype(jnp.bfloat16).reshape(panel_rows, PLAN_WIDTH, BLOCK)
        named_blocks = plan_blocks[panel_index].astype(jnp.int32)
        dense_plan = jnp.zeros((panel_rows, BLOCKS_B, BLOCK), jnp.float32).at[:, named_blocks].add(product.astype(jnp.float32)).astype(jnp.bfloat16)
        present = jnp.minimum(jnp.zeros((BLOCKS_B,), jnp.float32).at[named_blocks].add(jnp.float32(1.0)), jnp.float32(1.0))
        crossed = jnp.zeros((panel_rows, BLOCKS_B, BLOCK), jnp.float32)
        dense_wide = dense_plan.astype(jnp.float32)
        for neighbor in range(SECOND_NEAR):
            partial_sum = jnp.einsum("rkb,kbc->rkc", dense_wide, second_values[:, neighbor].astype(jnp.float32))
            targets = (panel_base + second_blocks[:, neighbor].astype(jnp.int32)).astype(jnp.int32)
            crossed = crossed.at[:, targets].add(partial_sum)
        kernel = present[None, :, None] * jnp.exp(crossed - offset_first[row_start:row_start + panel_rows][:, None, None] - offset_second[None])
        totals = jnp.sum(kernel, axis=(1, 2))
        row_scale = weight_first[row_start:row_start + panel_rows] * jnp.float32(plan_width) / totals
        weighted = kernel * row_scale[:, None, None]
        colsum = colsum + jnp.sum(weighted, axis=0)
        counts = counts + present * jnp.float32(panel_rows)
        kept_blocks.append(weighted[:, named_blocks, :])
        row_scales.append(row_scale)
    scale_second = weight_second * counts[:, None] / jnp.where(counts[:, None] > 0, colsum, jnp.float32(1.0))
    pieces = []
    for panel_index in range(PANELS):
        named_blocks = plan_blocks[panel_index].astype(jnp.int32)
        pieces.append((kept_blocks[panel_index] * scale_second[named_blocks][None]).astype(jnp.bfloat16))
    new_plan = jnp.concatenate(pieces, axis=0)
    scale_first = jnp.concatenate(row_scales, axis=0)
    return (new_plan, scale_first, scale_second)
```

```python
import functools
import jax
import jax.numpy as jnp
from jax import lax
from jax.experimental import pallas as pl
from jax.experimental.pallas import tpu as pltpu
from jax.sharding import PartitionSpec as P

LARGEST = float(jnp.finfo(jnp.bfloat16).max)


def params(mebibytes=40):
    return pltpu.CompilerParams(
        dimension_semantics=("arbitrary",), vmem_limit_bytes=mebibytes << 20
    )


def cost(flops, moved):
    return pl.CostEstimate(flops=flops, bytes_accessed=moved, transcendentals=0)


def first_kernel(near, x_ref, c_ref, o_ref, flat):
    step = pl.program_id(0)
    tiles, rows, width = flat.shape
    slots, half = x_ref.shape[1], x_ref.shape[2]
    chunk = o_ref.shape[2]

    @pl.when(step < tiles)
    def _():
        flat[step] = x_ref[...].reshape(rows, width)

    @pl.when(step >= tiles)
    def _():
        total = None
        for q in range(c_ref.shape[1]):
            term = jnp.dot(
                c_ref[0, q], flat[near[step - tiles, q]], preferred_element_type=jnp.float32
            )
            total = term if total is None else total + term
        total = total.astype(jnp.bfloat16)
        for part in range(o_ref.shape[0]):
            for slot in range(slots):
                o_ref[part, slot] = total[
                    part * chunk : (part + 1) * chunk, slot * half : (slot + 1) * half
                ]


def first_product(x, values, near, col_count):
    panel_rows, slots, half = x.shape
    tiles, count, rows, _ = values.shape
    chunk = panel_rows // col_count
    parts = rows // chunk

    def late(i, n):
        return (jnp.maximum(i - tiles, 0), 0, 0, 0)

    return pl.pallas_call(
        first_kernel,
        grid_spec=pltpu.PrefetchScalarGridSpec(
            num_scalar_prefetch=1,
            grid=(2 * tiles,),
            in_specs=[
                pl.BlockSpec((rows, slots, half), lambda i, n: (jnp.minimum(i, tiles - 1), 0, 0)),
                pl.BlockSpec((1, count, rows, rows), late),
            ],
            out_specs=pl.BlockSpec((parts, slots, chunk, half), late),
            scratch_shapes=[pltpu.VMEM((tiles, rows, slots * half), jnp.bfloat16)],
        ),
        out_shape=jax.ShapeDtypeStruct((col_count, slots, chunk, half), jnp.bfloat16),
        compiler_params=params(60),
        cost_estimate=cost(2 * panel_rows * count * rows * slots * half, 6 << 20),
        name="first_product",
    )(near, x, values)


def panel_kernel(near, place, v_ref, mine_ref, other_ref):
    block = pl.program_id(0)
    half = v_ref.shape[3]
    mine_ref[...] = jnp.zeros_like(mine_ref)
    other_ref[...] = jnp.zeros_like(other_ref)
    mine = pl.multiple_of(place[0] * half, half)
    other = pl.multiple_of((1 - place[0]) * half, half)
    for q in range(v_ref.shape[1]):
        target = pl.ds(pl.multiple_of(near[block, q] * half, half), half)
        mine_ref[:, target] = v_ref[0, q, pl.ds(mine, half), :]
        other_ref[:, target] = v_ref[0, q, pl.ds(other, half), :]


def panel_matrix(values, near, place):
    blocks, count, rows, half = values.shape
    out = pl.BlockSpec((half, blocks * half), lambda i, n, h: (i, 0))
    return pl.pallas_call(
        panel_kernel,
        grid_spec=pltpu.PrefetchScalarGridSpec(
            num_scalar_prefetch=2,
            grid=(blocks,),
            in_specs=[pl.BlockSpec((1, count, rows, half), lambda i, n, h: (i, 0, 0, 0))],
            out_specs=[out, out],
        ),
        out_shape=[jax.ShapeDtypeStruct((blocks * half, blocks * half), jnp.bfloat16)] * 2,
        compiler_params=params(),
        cost_estimate=cost(0, 8 << 20),
        name="panel_matrix",
    )(near, place, values)


def merge_kernel(ids, place, x_ref, o_ref, total):
    total[...] = jnp.zeros_like(total)
    slots = x_ref.shape[1]
    for step in range(x_ref.shape[0]):
        source = step ^ place[0]
        for slot in range(slots):
            total[ids[step * slots + slot]] += x_ref[source, slot].astype(jnp.float32)
    o_ref[...] = total[...].astype(jnp.bfloat16)


def merge(ids, place, x, block_count):
    sources, slots, rows, half = x.shape
    out = (block_count, rows, half)
    return pl.pallas_call(
        merge_kernel,
        grid_spec=pltpu.PrefetchScalarGridSpec(
            num_scalar_prefetch=2,
            grid=(1,),
            in_specs=[pl.BlockSpec(x.shape, lambda i, n, h: (0, 0, 0, 0))],
            out_specs=pl.BlockSpec(out, lambda i, n, h: (0, 0, 0)),
            scratch_shapes=[pltpu.VMEM(out, jnp.float32)],
        ),
        out_shape=jax.ShapeDtypeStruct(out, jnp.bfloat16),
        compiler_params=params(),
        cost_estimate=cost(0, 8 << 20),
        name="merge",
    )(ids, place, x)


def select_kernel(ids, place, x_ref, o_ref):
    slots = o_ref.shape[1]
    for step in range(o_ref.shape[0]):
        source = step ^ place[0]
        for slot in range(slots):
            o_ref[source, slot] = x_ref[ids[step * slots + slot]]


def select(ids, place, x, shape):
    return pl.pallas_call(
        select_kernel,
        grid_spec=pltpu.PrefetchScalarGridSpec(
            num_scalar_prefetch=2,
            grid=(1,),
            in_specs=[pl.BlockSpec(x.shape, lambda i, n, h: (0, 0, 0))],
            out_specs=pl.BlockSpec(shape, lambda i, n, h: (0, 0, 0, 0)),
        ),
        out_shape=pltpu.HBM(shape, jnp.bfloat16),
        compiler_params=params(),
        cost_estimate=cost(0, 4 << 20),
        name="select",
    )(ids, place, x)


def lay(x_ref, left):
    parts, blocks, chunk, half = x_ref.shape
    for part in range(parts):
        for block in range(blocks):
            left[part * chunk : (part + 1) * chunk, block * half : (block + 1) * half] = x_ref[
                part, block
            ]


def near_kernel(x_ref, m_ref, o_ref, left):
    lay(x_ref, left)
    o_ref[...] = jnp.dot(left[...], m_ref[...], preferred_element_type=jnp.float32)


def second_near(x, matrix, parts):
    col_count, blocks, chunk, half = x.shape
    depth, width = matrix.shape
    return pl.pallas_call(
        near_kernel,
        grid=(col_count // parts,),
        in_specs=[
            pl.BlockSpec((parts, blocks, chunk, half), lambda i: (i, 0, 0, 0)),
            pl.BlockSpec((depth, width), lambda i: (0, 0)),
        ],
        out_specs=pl.BlockSpec((parts * chunk, width), lambda i: (i, 0)),
        out_shape=jax.ShapeDtypeStruct((col_count * chunk, width), jnp.float32),
        scratch_shapes=[pltpu.VMEM((parts * chunk, depth), jnp.bfloat16)],
        compiler_params=params(),
        cost_estimate=cost(2 * col_count * chunk * depth * width, 8 << 20),
        name="second_near",
    )(x, matrix)


def far_kernel(x_ref, m_ref, near_ref, first_ref, second_ref, o_ref, sum_ref, left):
    parts, blocks, chunk, half = x_ref.shape
    lay(x_ref, left)
    first = jnp.broadcast_to(first_ref[...], (parts * chunk, half))
    partial = None
    for block in range(0, blocks, 2):
        columns = slice(block * half, (block + 2) * half)
        far = jnp.dot(left[...], m_ref[:, columns], preferred_element_type=jnp.float32)
        for side in range(2):
            own = slice((block + side) * half, (block + side + 1) * half)
            crossed = far[:, side * half : (side + 1) * half] + near_ref[:, own]
            value = jnp.exp(crossed - first - second_ref[:, own])
            partial = value if partial is None else partial + value
            rounded = jnp.minimum(value, LARGEST).astype(jnp.bfloat16)
            for part in range(parts):
                o_ref[part, block + side] = rounded[part * chunk : (part + 1) * chunk]
    sum_ref[0] = jnp.sum(partial.T, axis=0, keepdims=True)


def second_far(x, matrix, near, first, second, parts):
    col_count, blocks, chunk, half = x.shape
    steps = col_count // parts
    depth, width = matrix.shape
    data = pl.BlockSpec((parts, blocks, chunk, half), lambda i: (i, 0, 0, 0))
    return pl.pallas_call(
        far_kernel,
        grid=(steps,),
        in_specs=[
            data,
            pl.BlockSpec((depth, width), lambda i: (0, 0)),
            pl.BlockSpec((parts * chunk, width), lambda i: (i, 0)),
            pl.BlockSpec((parts * chunk, 1), lambda i: (i, 0)),
            pl.BlockSpec((1, width), lambda i: (0, 0)),
        ],
        out_specs=[data, pl.BlockSpec((1, 1, parts * chunk), lambda i: (i, 0, 0))],
        out_shape=[
            pltpu.HBM((col_count, blocks, chunk, half), jnp.bfloat16),
            jax.ShapeDtypeStruct((steps, 1, parts * chunk), jnp.float32),
        ],
        scratch_shapes=[pltpu.VMEM((parts * chunk, depth), jnp.bfloat16)],
        compiler_params=params(),
        cost_estimate=cost(2 * col_count * chunk * depth * width, 10 << 20),
        name="second_far",
    )(x, matrix, near, first, second)


def colsum_kernel(s_ref, x_ref, o_ref):
    parts, blocks, chunk, half = x_ref.shape
    for block in range(blocks):
        total = jnp.dot(
            s_ref[...],
            x_ref[:, block].reshape(parts * chunk, half),
            preferred_element_type=jnp.float32,
        )
        o_ref[block : block + 1] = total[0:1] + total[1:2] + total[2:3]


def weighted_colsum(scale, x):
    col_count, blocks, chunk, half = x.shape
    high = scale.astype(jnp.bfloat16)
    rest = scale - high.astype(jnp.float32)
    middle = rest.astype(jnp.bfloat16)
    low = (rest - middle.astype(jnp.float32)).astype(jnp.bfloat16)
    thirds = jnp.concatenate(
        [high[None], middle[None], low[None], jnp.zeros((13, scale.shape[0]), jnp.bfloat16)]
    )
    return pl.pallas_call(
        colsum_kernel,
        out_shape=jax.ShapeDtypeStruct((blocks, half), jnp.float32),
        compiler_params=pltpu.CompilerParams(vmem_limit_bytes=48 * 1024 * 1024),
        cost_estimate=cost(2 * 16 * col_count * blocks * chunk * half, 4 << 20),
        name="weighted_colsum",
    )(thirds, x)


def final_kernel(lines, x_ref, first_ref, second_ref, o_ref):
    parts, slots, chunk, half = x_ref.shape
    for part in range(parts):
        rows = slice(part * chunk, (part + 1) * chunk)
        first = jnp.broadcast_to(first_ref[rows, :], (chunk, half))
        values = [
            x_ref[part, slot].astype(jnp.float32) * first * second_ref[pl.ds(lines[slot], 1), :]
            for slot in range(slots)
        ]
        o_ref[rows] = jnp.swapaxes(jnp.stack(values), 0, 1).astype(jnp.bfloat16)


def final_scale(named, x, first, second, parts):
    col_count, slots, chunk, half = x.shape
    steps = col_count // parts
    return pl.pallas_call(
        final_kernel,
        grid_spec=pltpu.PrefetchScalarGridSpec(
            num_scalar_prefetch=1,
            grid=(steps,),
            in_specs=[
                pl.BlockSpec((parts, slots, chunk, half), lambda i, n: (i, 0, 0, 0)),
                pl.BlockSpec((parts * chunk, 1), lambda i, n: (i, 0)),
                pl.BlockSpec(second.shape, lambda i, n: (0, 0)),
            ],
            out_specs=pl.BlockSpec((parts * chunk, slots, half), lambda i, n: (i, 0, 0)),
        ),
        out_shape=jax.ShapeDtypeStruct((col_count * chunk, slots, half), jnp.bfloat16),
        compiler_params=params(),
        cost_estimate=cost(0, 5 << 20),
        name="final_scale",
    )(named, x, first, second)


def swap(value, axis, bit):
    size = lax.axis_size(axis)
    return lax.ppermute(value, axis, [(i, i ^ bit) for i in range(size)])


def step_row(value, by, bits):
    rows, cols = lax.axis_size("row"), lax.axis_size("col")
    pairs = [
        (r * cols + c, (r + by) % rows * cols + (c ^ bits))
        for r in range(rows)
        for c in range(cols)
    ]
    return lax.ppermute(value, ("row", "col"), pairs)


def four(value, low, by, same):
    own = value if same else step_row(value, by, 0)
    return [own] + [step_row(value, by, k * low) for k in (1, 2, 3)]


def local(
    plan_values,
    plan_blocks,
    first_values,
    first_blocks,
    second_values,
    second_blocks,
    weight_first,
    weight_second,
    offset_first,
    offset_second,
):
    col_count = lax.axis_size("col")
    column = lax.axis_index("col")
    side = lax.axis_index("pan")
    blocks_here = second_blocks.shape[0]
    panel_rows, slots, half = plan_values.shape
    block_size = first_values.shape[2]
    chunk = panel_rows // col_count
    plan_width = float(slots * col_count * block_size)
    block_count = blocks_here * col_count

    named = plan_blocks[0]
    place = column.reshape(1)
    product = first_product(plan_values, first_values, first_blocks, col_count)
    arrived = lax.all_to_all(product, "col", split_axis=0, concat_axis=0, tiled=True)
    ids = jnp.concatenate(four(named, 1, 1, False))
    ids = jnp.concatenate(four(ids, 4, -1, False))
    matrix_mine, matrix_other = panel_matrix(second_values, second_blocks, side.reshape(1))
    own_blocks = column * blocks_here + jnp.arange(blocks_here)
    present = jnp.any(ids[:, None] == own_blocks[None, :], axis=0)
    ids, matrix_mine, matrix_other = lax.optimization_barrier((ids, matrix_mine, matrix_other))
    merged = merge(ids, place, arrived, block_count)
    merged = merged.reshape(col_count, blocks_here, chunk, half)
    mine = lax.all_to_all(merged, "col", split_axis=0, concat_axis=0, tiled=True)
    other = swap(mine, "pan", 1)
    near = second_near(mine, matrix_mine, 8)
    offsets = jnp.where(present[:, None], offset_second, jnp.inf).reshape(1, -1)
    kernel, totals = second_far(other, matrix_other, near, offset_first[:, None], offsets, 8)
    back = lax.all_to_all(kernel, "col", split_axis=0, concat_axis=0, tiled=True)

    totals = totals.reshape(blocks_here, -1)
    totals = totals + swap(totals, "pan", 1)
    for low, by in ((1, 1), (4, -1)):
        own, one, two, three = four(totals, low, by, False)
        totals = (own + one) + (two + three)
    scale_first = weight_first * plan_width / totals.reshape(-1)
    colsum = weighted_colsum(scale_first, kernel)
    sums = jnp.concatenate(
        [colsum, jnp.broadcast_to(present.astype(jnp.float32)[:, None], colsum.shape)]
    )
    for bit in (1, 2, 4):
        sums = sums + swap(sums, "row", bit)
    colsum = sums[:blocks_here]
    counts = sums[blocks_here:, :1] * float(panel_rows)
    scale_second = weight_second * counts / jnp.where(counts > 0, colsum, 1.0)
    all_second = jnp.concatenate(four(scale_second, 1, 1, True))
    all_second = jnp.concatenate(four(all_second, 4, 1, True))
    lines = ((named // blocks_here) ^ column) * blocks_here + named % blocks_here

    chosen = select(ids, place, back.reshape(block_count, chunk, half), product.shape)
    home = lax.all_to_all(chosen, "col", split_axis=0, concat_axis=0, tiled=True)
    new_plan = final_scale(lines, home, scale_first[:, None], all_second, 4)
    return (new_plan, scale_first, scale_second)


def solution(mesh):
    return jax.shard_map(
        local,
        mesh=mesh,
        in_specs=(
            P("row", "col", "pan"),
            P("row", "col"),
            P("row", None, None, None),
            P("row", None),
            P("col", None, None, "pan"),
            P("col", None),
            P("row"),
            P("col", "pan"),
            P("row"),
            P("col", "pan"),
        ),
        out_specs=(P("row", "col", "pan"), P("row"), P("col", "pan")),
        check_vma=False,
    )
```

```python
import functools
import jax
import jax.numpy as jnp
from jax import lax
from jax.experimental import pallas as pl
from jax.experimental.pallas import tpu as pltpu
from jax.sharding import PartitionSpec as P

LARGEST = float(jnp.finfo(jnp.bfloat16).max)


def params(mebibytes=40):
    return pltpu.CompilerParams(
        dimension_semantics=("arbitrary",), vmem_limit_bytes=mebibytes << 20
    )


def cost(flops, moved):
    return pl.CostEstimate(flops=flops, bytes_accessed=moved, transcendentals=0)


VMEM = pl.BlockSpec(memory_space=pltpu.VMEM)
SMEM = pl.BlockSpec(memory_space=pltpu.SMEM)
ANY = pl.BlockSpec(memory_space=pl.ANY)


def first_kernel(near, named, x_hbm, c_hbm, o_hbm, x, c, flat, out, x_sem, c_sem, o_sem):
    tiles, count, rows, _ = c.shape
    slots, half = x.shape[1:]
    chunk = x.shape[0] // out.shape[0]
    parts = rows // chunk

    def load_x(tile):
        part = pl.ds(tile * rows, rows)
        return pltpu.make_async_copy(x_hbm.at[part], x.at[part], x_sem.at[tile])

    def load_c(tile):
        return pltpu.make_async_copy(c_hbm.at[tile], c.at[tile], c_sem.at[tile])

    def store(tile):
        part = pl.ds(tile * parts, parts)
        return pltpu.make_async_copy(out.at[part], o_hbm.at[part], o_sem.at[tile])

    for tile in range(tiles):
        load_x(tile).start()
    for tile in range(tiles):
        load_c(tile).start()
    lanes = lax.broadcasted_iota(jnp.int32, (8, half), 1)
    line = jnp.zeros((8, half), jnp.int32)
    for slot in range(slots):
        line = jnp.where(lanes == slot, named[slot], line)
    for part in range(out.shape[0]):
        out[part, slots * chunk :] = line.astype(jnp.float32).astype(jnp.bfloat16)
    for tile in range(tiles):
        load_x(tile).wait()
        flat[tile] = x[tile * rows : (tile + 1) * rows].reshape(rows, slots * half)
    for tile in range(tiles):
        load_c(tile).wait()
        total = None
        for q in range(count):
            term = jnp.dot(c[tile, q], flat[near[tile, q]], preferred_element_type=jnp.float32)
            total = term if total is None else total + term
        total = total.astype(jnp.bfloat16)
        for part in range(parts):
            for slot in range(slots):
                out[tile * parts + part, slot * chunk : (slot + 1) * chunk] = total[
                    part * chunk : (part + 1) * chunk, slot * half : (slot + 1) * half
                ]
        store(tile).start()
    for tile in range(tiles):
        store(tile).wait()


def first_product(x, values, near, named, col_count):
    panel_rows, slots, half = x.shape
    tiles, count, rows, _ = values.shape
    chunk = panel_rows // col_count
    shape = (col_count, slots * chunk + 8, half)
    return pl.pallas_call(
        first_kernel,
        in_specs=[SMEM, SMEM, ANY, ANY],
        out_specs=ANY,
        out_shape=pltpu.HBM(shape, jnp.bfloat16),
        scratch_shapes=[
            pltpu.VMEM(x.shape, jnp.bfloat16),
            pltpu.VMEM(values.shape, jnp.bfloat16),
            pltpu.VMEM((tiles, rows, slots * half), jnp.bfloat16),
            pltpu.VMEM(shape, jnp.bfloat16),
            pltpu.SemaphoreType.DMA((tiles,)),
            pltpu.SemaphoreType.DMA((tiles,)),
            pltpu.SemaphoreType.DMA((tiles,)),
        ],
        compiler_params=pltpu.CompilerParams(vmem_limit_bytes=60 << 20),
        cost_estimate=cost(2 * panel_rows * count * rows * slots * half, 6 << 20),
        name="first_product",
    )(near, named, x, values)


def merge_kernel(x_ref, o_ref, ids_ref, total, ids, sem):
    sources, height, half = x_ref.shape
    _, chunk, width = o_ref.shape
    slots = (height - 8) // chunk
    ids_ref[...] = x_ref[:, height - 8 :].astype(jnp.float32)[:, 0].astype(jnp.int32)
    copy = pltpu.make_async_copy(ids_ref, ids, sem)
    copy.start()
    total[...] = jnp.zeros_like(total)
    copy.wait()
    for source in range(sources):
        for slot in range(slots):
            piece = x_ref[source, slot * chunk : (slot + 1) * chunk]
            total[ids[source, slot]] += piece.astype(jnp.float32)
    blocks = width // half
    for panel in range(o_ref.shape[0]):
        for block in range(blocks):
            o_ref[panel, :, block * half : (block + 1) * half] = total[
                panel * blocks + block
            ].astype(jnp.bfloat16)


def merge(x, panels, blocks, chunk):
    sources, _, half = x.shape
    return pl.pallas_call(
        merge_kernel,
        in_specs=[VMEM],
        out_specs=[VMEM, VMEM],
        out_shape=[
            jax.ShapeDtypeStruct((panels, chunk, blocks * half), jnp.bfloat16),
            jax.ShapeDtypeStruct((sources, half), jnp.int32),
        ],
        scratch_shapes=[
            pltpu.VMEM((panels * blocks, chunk, half), jnp.float32),
            pltpu.SMEM((sources, half), jnp.int32),
            pltpu.SemaphoreType.DMA,
        ],
        compiler_params=pltpu.CompilerParams(vmem_limit_bytes=40 << 20),
        cost_estimate=cost(0, 8 << 20),
        name="merge",
    )(x)


def select_kernel(ids, x_ref, o_hbm, out, sem):
    sources, slots, chunk, half = out.shape
    blocks = x_ref.shape[2] // half
    groups = sem.shape[0]
    size = sources // groups

    def store(group):
        part = pl.ds(group * size, size)
        return pltpu.make_async_copy(out.at[part], o_hbm.at[part], sem.at[group])

    for group in range(groups):
        for source in range(group * size, (group + 1) * size):
            for slot in range(slots):
                block = ids[source * slots + slot]
                lanes = pl.ds(pl.multiple_of(lax.rem(block, blocks) * half, half), half)
                out[source, slot] = x_ref[lax.div(block, blocks), :, lanes]
        store(group).start()
    for group in range(groups):
        store(group).wait()


def select(ids, x, slots, half):
    sources, chunk, _ = x.shape
    shape = (sources, slots, chunk, half)
    return pl.pallas_call(
        select_kernel,
        in_specs=[SMEM, VMEM],
        out_specs=ANY,
        out_shape=pltpu.HBM(shape, jnp.bfloat16),
        scratch_shapes=[pltpu.VMEM(shape, jnp.bfloat16), pltpu.SemaphoreType.DMA((4,))],
        compiler_params=pltpu.CompilerParams(vmem_limit_bytes=40 << 20),
        cost_estimate=cost(0, 4 << 20),
        name="select",
    )(ids, x)


def near_kernel(near, place, x_ref, v_hbm, o_ref, other_ref, v, mine_ref, sem):
    parts, chunk, depth = x_ref.shape
    blocks, count, rows, half = v.shape

    def load(block):
        return pltpu.make_async_copy(v_hbm.at[block], v.at[block], sem.at[block])

    for block in range(blocks):
        load(block).start()
    mine_ref[...] = jnp.zeros_like(mine_ref)
    other_ref[...] = jnp.zeros_like(other_ref)
    mine = pl.multiple_of(place[0] * half, half)
    other = pl.multiple_of((1 - place[0]) * half, half)
    for block in range(blocks):
        load(block).wait()
        own = slice(block * half, (block + 1) * half)
        for q in range(count):
            target = pl.ds(pl.multiple_of(near[block, q] * half, half), half)
            mine_ref[own, target] = v[block, q, pl.ds(mine, half), :]
            other_ref[own, target] = v[block, q, pl.ds(other, half), :]
    side = parts // 2
    for part in range(2):
        o_ref[part * side * chunk : (part + 1) * side * chunk] = jnp.dot(
            x_ref[part * side : (part + 1) * side].reshape(side * chunk, depth),
            mine_ref[...],
            preferred_element_type=jnp.float32,
        )


def second_near(x, values, near, place):
    parts, chunk, depth = x.shape
    blocks, count, rows, half = values.shape
    columns = blocks * half
    return pl.pallas_call(
        near_kernel,
        in_specs=[SMEM, SMEM, VMEM, ANY],
        out_specs=[VMEM, VMEM],
        out_shape=[
            jax.ShapeDtypeStruct((parts * chunk, columns), jnp.float32),
            jax.ShapeDtypeStruct((depth, columns), jnp.bfloat16),
        ],
        scratch_shapes=[
            pltpu.VMEM(values.shape, jnp.bfloat16),
            pltpu.VMEM((depth, columns), jnp.bfloat16),
            pltpu.SemaphoreType.DMA((blocks,)),
        ],
        compiler_params=pltpu.CompilerParams(vmem_limit_bytes=40 << 20),
        cost_estimate=cost(2 * parts * chunk * depth * columns, 8 << 20),
        name="second_near",
    )(near, place, x, pltpu.with_memory_space_constraint(values, pltpu.HBM))


def far_kernel(x_ref, m_ref, near_ref, first_ref, second_ref, o_ref, sum_ref):
    parts, chunk, columns = o_ref.shape
    rows, half = parts * chunk, 128
    step = pl.program_id(0)
    left = x_ref[pl.ds(step * parts, parts)].reshape(rows, x_ref.shape[2])
    own = pl.ds(pl.multiple_of(step * rows, rows), rows)
    first = jnp.broadcast_to(first_ref[own, :], (rows, half))
    partial = None
    for pair in range(0, columns, 2 * half):
        far = jnp.dot(left, m_ref[:, pair : pair + 2 * half], preferred_element_type=jnp.float32)
        for at in (0, half):
            lanes = slice(pair + at, pair + at + half)
            value = jnp.exp(
                far[:, at : at + half] + near_ref[own, lanes] - first - second_ref[:, lanes]
            )
            partial = value if partial is None else partial + value
            rounded = jnp.minimum(value, LARGEST).astype(jnp.bfloat16)
            o_ref[:, :, lanes] = rounded.reshape(parts, chunk, half)
    sum_ref[0] = jnp.sum(partial.T, axis=0, keepdims=True)


def second_far(x, matrix, near, first, second, parts):
    col_count, chunk, depth = x.shape
    rows = parts * chunk
    columns = matrix.shape[1]
    steps = col_count // parts
    return pl.pallas_call(
        far_kernel,
        grid=(steps,),
        in_specs=[VMEM] * 5,
        out_specs=[
            pl.BlockSpec((parts, chunk, columns), lambda i: (i, 0, 0)),
            pl.BlockSpec((1, 1, rows), lambda i: (i, 0, 0)),
        ],
        out_shape=[
            pltpu.HBM((col_count, chunk, columns), jnp.bfloat16),
            jax.ShapeDtypeStruct((steps, 1, rows), jnp.float32),
        ],
        compiler_params=params(),
        cost_estimate=cost(2 * col_count * chunk * depth * columns, 10 << 20),
        name="second_far",
    )(x, matrix, near, first, second)


def colsum_kernel(s_ref, x_hbm, o_ref, x, sem):
    groups = sem.shape[0]
    parts, chunk, width = x.shape
    size = parts // groups

    def load(group):
        part = pl.ds(group * size, size)
        return pltpu.make_async_copy(x_hbm.at[part], x.at[part], sem.at[group])

    for group in range(groups):
        load(group).start()
    total = None
    for group in range(groups):
        load(group).wait()
        rows = slice(group * size * chunk, (group + 1) * size * chunk)
        term = jnp.dot(
            s_ref[:, rows],
            x[group * size : (group + 1) * size].reshape(size * chunk, width),
            preferred_element_type=jnp.float32,
        )
        total = term if total is None else total + term
    blocks, half = o_ref.shape
    line = total[0:1] + total[1:2] + total[2:3]
    for block in range(blocks):
        o_ref[block : block + 1] = line[:, block * half : (block + 1) * half]


def weighted_colsum(scale, x, blocks):
    parts, chunk, width = x.shape
    high = scale.astype(jnp.bfloat16)
    rest = scale - high.astype(jnp.float32)
    middle = rest.astype(jnp.bfloat16)
    low = (rest - middle.astype(jnp.float32)).astype(jnp.bfloat16)
    thirds = jnp.concatenate(
        [high[None], middle[None], low[None], jnp.zeros((13, scale.shape[0]), jnp.bfloat16)]
    )
    return pl.pallas_call(
        colsum_kernel,
        in_specs=[VMEM, ANY],
        out_specs=VMEM,
        out_shape=jax.ShapeDtypeStruct((blocks, width // blocks), jnp.float32),
        scratch_shapes=[pltpu.VMEM(x.shape, jnp.bfloat16), pltpu.SemaphoreType.DMA((4,))],
        compiler_params=pltpu.CompilerParams(vmem_limit_bytes=40 << 20),
        cost_estimate=cost(2 * 16 * parts * chunk * width, 4 << 20),
        name="weighted_colsum",
    )(thirds, pltpu.with_memory_space_constraint(x, pltpu.HBM))


def final_kernel(lines, x_ref, first_ref, second_ref, o_ref):
    step = pl.program_id(0)
    rows, slots, half = o_ref.shape
    chunk = x_ref.shape[2]
    for part in range(rows // chunk):
        at = step * (rows // chunk) + part
        first = first_ref[pl.ds(pl.multiple_of(at * chunk, chunk), chunk), :]
        first = jnp.broadcast_to(first, (chunk, half))
        values = [
            x_ref[at, slot].astype(jnp.float32) * first * second_ref[pl.ds(lines[slot], 1), :]
            for slot in range(slots)
        ]
        o_ref[part * chunk : (part + 1) * chunk] = jnp.swapaxes(jnp.stack(values), 0, 1).astype(
            jnp.bfloat16
        )


def final_scale(lines, x, first, second, parts):
    col_count, slots, chunk, half = x.shape
    steps = col_count // parts
    return pl.pallas_call(
        final_kernel,
        grid_spec=pltpu.PrefetchScalarGridSpec(
            num_scalar_prefetch=1,
            grid=(steps,),
            in_specs=[VMEM, VMEM, VMEM],
            out_specs=pl.BlockSpec((parts * chunk, slots, half), lambda i, n: (i, 0, 0)),
        ),
        out_shape=pltpu.HBM((col_count * chunk, slots, half), jnp.bfloat16),
        compiler_params=params(),
        cost_estimate=cost(0, 5 << 20),
        name="final_scale",
    )(lines, x, first, second)


def swap(value, axis, bit):
    size = lax.axis_size(axis)
    return lax.ppermute(value, axis, [(i, i ^ bit) for i in range(size)])


def move(value, by, bits):
    rows, cols, cores = (lax.axis_size(axis) for axis in ("row", "col", "pan"))
    pairs = [
        ((r * cols + c) * cores + h, ((r + by) % rows * cols + (c ^ bits[h])) * cores + h)
        for r in range(rows)
        for c in range(cols)
        for h in range(cores)
    ]
    return lax.ppermute(value, ("row", "col", "pan"), pairs)


def four(value, low, by):
    return [value] + [move(value, by, (k * low, k * low)) for k in (1, 2, 3)]


def shared_pairs(value, low, by):
    return move(value, by, (0, low)), move(value, by, (2 * low, 3 * low))


def shared_sum(value, low, by):
    first, second = shared_pairs(value, low, by)
    both = first + second
    return both + swap(both, "pan", 1)


def local(
    plan_values,
    plan_blocks,
    first_values,
    first_blocks,
    second_values,
    second_blocks,
    weight_first,
    weight_second,
    offset_first,
    offset_second,
):
    col_count = lax.axis_size("col")
    column = lax.axis_index("col")
    side = lax.axis_index("pan")
    blocks_here = second_blocks.shape[0]
    panel_rows, slots, half = plan_values.shape
    block_size = first_values.shape[2]
    chunk = panel_rows // col_count
    plan_width = float(slots * col_count * block_size)

    named = plan_blocks[0]
    product = first_product(plan_values, first_values, first_blocks, named, col_count)
    arrived = lax.all_to_all(product, "col", split_axis=0, concat_axis=0, tiled=True)
    merged, ids = merge(arrived, col_count, blocks_here, chunk)
    merged, offset_first, offset_second = lax.optimization_barrier(
        (merged, offset_first, offset_second)
    )
    mine = lax.all_to_all(merged, "col", split_axis=0, concat_axis=0, tiled=True)
    ids = ids[:, :slots].reshape(-1)
    own_blocks = column * blocks_here + jnp.arange(blocks_here)
    present = jnp.any(ids[:, None] == own_blocks[None, :], axis=0)
    other = swap(mine, "pan", 1)
    near, matrix_other = second_near(mine, second_values, second_blocks, side.reshape(1))
    offsets = jnp.where(present[:, None], offset_second, jnp.inf).reshape(1, -1)
    kernel, totals = second_far(other, matrix_other, near, offset_first[:, None], offsets, 8)
    back = lax.all_to_all(kernel, "col", split_axis=0, concat_axis=0, tiled=True)

    totals = totals.reshape(blocks_here, -1)
    totals = totals + swap(totals, "pan", 1)
    totals = shared_sum(totals, 1, 1)
    totals = shared_sum(totals, 4, -1)
    scale_first = weight_first * plan_width / totals.reshape(-1)
    colsum = weighted_colsum(scale_first, kernel, blocks_here)
    sums = jnp.concatenate(
        [colsum, jnp.broadcast_to(present.astype(jnp.float32)[:, None], colsum.shape)]
    )
    sums = sums + swap(sums, "row", 1)
    sums = sums + swap(sums, "row", 2)
    ids, sums = lax.optimization_barrier((ids, sums))
    sums = sums + swap(sums, "row", 7)
    colsum = sums[:blocks_here]
    counts = sums[blocks_here:, :1] * float(panel_rows)
    scale_second = weight_second * counts / jnp.where(counts > 0, colsum, 1.0)
    all_second = jnp.concatenate(four(scale_second, 1, 1))
    all_second = jnp.concatenate(four(all_second, 4, 1))
    lines = ((named // blocks_here) ^ column) * blocks_here + named % blocks_here

    chosen = select(ids, back, slots, half)
    home = lax.all_to_all(chosen, "col", split_axis=0, concat_axis=0, tiled=True)
    new_plan = final_scale(lines, home, scale_first[:, None], all_second, 4)
    return (new_plan, scale_first, scale_second)


def solution(mesh):
    return jax.shard_map(
        local,
        mesh=mesh,
        in_specs=(
            P("row", "col", "pan"),
            P("row", "col"),
            P("row", None, None, None),
            P("row", None),
            P("col", None, None, "pan"),
            P("col", None),
            P("row"),
            P("col", "pan"),
            P("row"),
            P("col", "pan"),
        ),
        out_specs=(P("row", "col", "pan"), P("row"), P("col", "pan")),
        check_vma=False,
    )
```

```python
import functools
import jax
import jax.numpy as jnp
from jax import lax
from jax.experimental import pallas as pl
from jax.experimental.pallas import tpu as pltpu
from jax.sharding import PartitionSpec as P

LARGEST = float(jnp.finfo(jnp.bfloat16).max)


def params(mebibytes=40):
    return pltpu.CompilerParams(
        dimension_semantics=("arbitrary",), vmem_limit_bytes=mebibytes << 20
    )


def cost(flops, moved):
    return pl.CostEstimate(flops=flops, bytes_accessed=moved, transcendentals=0)


VMEM = pl.BlockSpec(memory_space=pltpu.VMEM)
SMEM = pl.BlockSpec(memory_space=pltpu.SMEM)
ANY = pl.BlockSpec(memory_space=pl.ANY)


def first_kernel(place, near, named, x_hbm, c_hbm, o_hbm, x, c, flat, out, x_sem, c_sem, o_sem):
    tiles, count, rows, _ = c.shape
    slots, half = x.shape[1:]
    chunk = x.shape[0] // out.shape[0]
    parts = rows // chunk

    def load_x(tile):
        part = pl.ds(tile * rows, rows)
        return pltpu.make_async_copy(x_hbm.at[part], x.at[part], x_sem.at[tile])

    def load_c(tile):
        return pltpu.make_async_copy(c_hbm.at[tile], c.at[tile], c_sem.at[tile])

    def store(tile):
        part = pl.ds(tile * parts, parts)
        return pltpu.make_async_copy(out.at[part], o_hbm.at[part], o_sem.at[tile])

    for tile in range(tiles):
        load_x(tile).start()
    for tile in range(tiles):
        load_c(tile).start()
    lanes = lax.broadcasted_iota(jnp.int32, (8, half), 1)
    line = jnp.zeros((8, half), jnp.int32)
    for slot in range(slots):
        line = jnp.where(lanes == slot, named[slot], line)
    for part in range(out.shape[0]):
        out[part, slots * chunk :] = line.astype(jnp.float32).astype(jnp.bfloat16)
    for tile in range(tiles):
        load_x(tile).wait()
        flat[tile] = x[tile * rows : (tile + 1) * rows].reshape(rows, slots * half)
    for tile in range(tiles):
        load_c(tile).wait()
        total = None
        for q in range(count):
            term = jnp.dot(c[tile, q], flat[near[tile, q]], preferred_element_type=jnp.float32)
            total = term if total is None else total + term
        total = total.astype(jnp.bfloat16)
        for part in range(parts):
            for slot in range(slots):
                out[tile * parts + part, slot * chunk : (slot + 1) * chunk] = total[
                    part * chunk : (part + 1) * chunk, slot * half : (slot + 1) * half
                ]
        store(tile).start()
    for tile in range(tiles):
        store(tile).wait()

    @pl.when(place[0] == 1)
    def _():
        pl.delay(12000)


def first_product(x, values, near, named, place, col_count):
    panel_rows, slots, half = x.shape
    tiles, count, rows, _ = values.shape
    chunk = panel_rows // col_count
    shape = (col_count, slots * chunk + 8, half)
    return pl.pallas_call(
        first_kernel,
        in_specs=[SMEM, SMEM, SMEM, ANY, ANY],
        out_specs=ANY,
        out_shape=pltpu.HBM(shape, jnp.bfloat16),
        scratch_shapes=[
            pltpu.VMEM(x.shape, jnp.bfloat16),
            pltpu.VMEM(values.shape, jnp.bfloat16),
            pltpu.VMEM((tiles, rows, slots * half), jnp.bfloat16),
            pltpu.VMEM(shape, jnp.bfloat16),
            pltpu.SemaphoreType.DMA((tiles,)),
            pltpu.SemaphoreType.DMA((tiles,)),
            pltpu.SemaphoreType.DMA((tiles,)),
        ],
        compiler_params=pltpu.CompilerParams(vmem_limit_bytes=60 << 20),
        cost_estimate=cost(2 * panel_rows * count * rows * slots * half, 6 << 20),
        name="first_product",
    )(place, near, named, x, values)


def merge_kernel(x_ref, o_ref, ids_ref, total, ids, sem):
    sources, height, half = x_ref.shape
    _, chunk, width = o_ref.shape
    slots = (height - 8) // chunk
    ids_ref[...] = x_ref[:, height - 8 :].astype(jnp.float32)[:, 0].astype(jnp.int32)
    copy = pltpu.make_async_copy(ids_ref, ids, sem)
    copy.start()
    total[...] = jnp.zeros_like(total)
    copy.wait()
    for source in range(sources):
        for slot in range(slots):
            piece = x_ref[source, slot * chunk : (slot + 1) * chunk]
            total[ids[source, slot]] += piece.astype(jnp.float32)
    blocks = width // half
    for panel in range(o_ref.shape[0]):
        for block in range(blocks):
            o_ref[panel, :, block * half : (block + 1) * half] = total[
                panel * blocks + block
            ].astype(jnp.bfloat16)


def merge(x, panels, blocks, chunk):
    sources, _, half = x.shape
    return pl.pallas_call(
        merge_kernel,
        in_specs=[VMEM],
        out_specs=[VMEM, VMEM],
        out_shape=[
            jax.ShapeDtypeStruct((panels, chunk, blocks * half), jnp.bfloat16),
            jax.ShapeDtypeStruct((sources, half), jnp.int32),
        ],
        scratch_shapes=[
            pltpu.VMEM((panels * blocks, chunk, half), jnp.float32),
            pltpu.SMEM((sources, half), jnp.int32),
            pltpu.SemaphoreType.DMA,
        ],
        compiler_params=pltpu.CompilerParams(vmem_limit_bytes=40 << 20),
        cost_estimate=cost(0, 8 << 20),
        name="merge",
    )(x)


def select_kernel(ids, x_ref, o_hbm, out, sem):
    sources, slots, chunk, half = out.shape
    blocks = x_ref.shape[2] // half
    groups = sem.shape[0]
    size = sources // groups

    def store(group):
        part = pl.ds(group * size, size)
        return pltpu.make_async_copy(out.at[part], o_hbm.at[part], sem.at[group])

    for group in range(groups):
        for source in range(group * size, (group + 1) * size):
            for slot in range(slots):
                block = ids[source * slots + slot]
                lanes = pl.ds(pl.multiple_of(lax.rem(block, blocks) * half, half), half)
                out[source, slot] = x_ref[lax.div(block, blocks), :, lanes]
        store(group).start()
    for group in range(groups):
        store(group).wait()


def select(ids, x, slots, half):
    sources, chunk, _ = x.shape
    shape = (sources, slots, chunk, half)
    return pl.pallas_call(
        select_kernel,
        in_specs=[SMEM, VMEM],
        out_specs=ANY,
        out_shape=pltpu.HBM(shape, jnp.bfloat16),
        scratch_shapes=[pltpu.VMEM(shape, jnp.bfloat16), pltpu.SemaphoreType.DMA((4,))],
        compiler_params=pltpu.CompilerParams(vmem_limit_bytes=40 << 20),
        cost_estimate=cost(0, 4 << 20),
        name="select",
    )(ids, x)


def near_kernel(near, place, x_ref, v_hbm, o_ref, other_ref, v, mine_ref, sem):
    parts, chunk, depth = x_ref.shape
    blocks, count, rows, half = v.shape

    def load(block):
        return pltpu.make_async_copy(v_hbm.at[block], v.at[block], sem.at[block])

    for block in range(blocks):
        load(block).start()
    mine_ref[...] = jnp.zeros_like(mine_ref)
    other_ref[...] = jnp.zeros_like(other_ref)
    mine = pl.multiple_of(place[0] * half, half)
    other = pl.multiple_of((1 - place[0]) * half, half)
    for block in range(blocks):
        load(block).wait()
        own = slice(block * half, (block + 1) * half)
        for q in range(count):
            target = pl.ds(pl.multiple_of(near[block, q] * half, half), half)
            mine_ref[own, target] = v[block, q, pl.ds(mine, half), :]
            other_ref[own, target] = v[block, q, pl.ds(other, half), :]
    side = parts // 2
    for part in range(2):
        o_ref[part * side * chunk : (part + 1) * side * chunk] = jnp.dot(
            x_ref[part * side : (part + 1) * side].reshape(side * chunk, depth),
            mine_ref[...],
            preferred_element_type=jnp.float32,
        )


def second_near(x, values, near, place):
    parts, chunk, depth = x.shape
    blocks, count, rows, half = values.shape
    columns = blocks * half
    return pl.pallas_call(
        near_kernel,
        in_specs=[SMEM, SMEM, VMEM, ANY],
        out_specs=[VMEM, VMEM],
        out_shape=[
            jax.ShapeDtypeStruct((parts * chunk, columns), jnp.float32),
            jax.ShapeDtypeStruct((depth, columns), jnp.bfloat16),
        ],
        scratch_shapes=[
            pltpu.VMEM(values.shape, jnp.bfloat16),
            pltpu.VMEM((depth, columns), jnp.bfloat16),
            pltpu.SemaphoreType.DMA((blocks,)),
        ],
        compiler_params=pltpu.CompilerParams(vmem_limit_bytes=40 << 20),
        cost_estimate=cost(2 * parts * chunk * depth * columns, 8 << 20),
        name="second_near",
    )(near, place, x, pltpu.with_memory_space_constraint(values, pltpu.HBM))


def far_kernel(x_ref, m_ref, near_ref, first_ref, second_ref, o_ref, sum_ref):
    parts, chunk, columns = o_ref.shape
    rows, half = parts * chunk, 128
    step = pl.program_id(0)
    left = x_ref[pl.ds(step * parts, parts)].reshape(rows, x_ref.shape[2])
    own = pl.ds(pl.multiple_of(step * rows, rows), rows)
    first = jnp.broadcast_to(first_ref[own, :], (rows, half))
    partial = None
    for pair in range(0, columns, 2 * half):
        far = jnp.dot(left, m_ref[:, pair : pair + 2 * half], preferred_element_type=jnp.float32)
        for at in (0, half):
            lanes = slice(pair + at, pair + at + half)
            value = jnp.exp(
                far[:, at : at + half] + near_ref[own, lanes] - first - second_ref[:, lanes]
            )
            partial = value if partial is None else partial + value
            rounded = jnp.minimum(value, LARGEST).astype(jnp.bfloat16)
            o_ref[:, :, lanes] = rounded.reshape(parts, chunk, half)
    sum_ref[0] = jnp.sum(partial.T, axis=0, keepdims=True)


def second_far(x, matrix, near, first, second, parts):
    col_count, chunk, depth = x.shape
    rows = parts * chunk
    columns = matrix.shape[1]
    steps = col_count // parts
    return pl.pallas_call(
        far_kernel,
        grid=(steps,),
        in_specs=[VMEM] * 5,
        out_specs=[
            pl.BlockSpec((parts, chunk, columns), lambda i: (i, 0, 0)),
            pl.BlockSpec((1, 1, rows), lambda i: (i, 0, 0)),
        ],
        out_shape=[
            pltpu.HBM((col_count, chunk, columns), jnp.bfloat16),
            jax.ShapeDtypeStruct((steps, 1, rows), jnp.float32),
        ],
        compiler_params=params(),
        cost_estimate=cost(2 * col_count * chunk * depth * columns, 10 << 20),
        name="second_far",
    )(x, matrix, near, first, second)


def colsum_kernel(s_ref, x_hbm, o_ref, x, sem):
    groups = sem.shape[0]
    parts, chunk, width = x.shape
    size = parts // groups

    def load(group):
        part = pl.ds(group * size, size)
        return pltpu.make_async_copy(x_hbm.at[part], x.at[part], sem.at[group])

    for group in range(groups):
        load(group).start()
    total = None
    for group in range(groups):
        load(group).wait()
        rows = slice(group * size * chunk, (group + 1) * size * chunk)
        term = jnp.dot(
            s_ref[:, rows],
            x[group * size : (group + 1) * size].reshape(size * chunk, width),
            preferred_element_type=jnp.float32,
        )
        total = term if total is None else total + term
    blocks, half = o_ref.shape
    line = total[0:1] + total[1:2] + total[2:3]
    for block in range(blocks):
        o_ref[block : block + 1] = line[:, block * half : (block + 1) * half]


def weighted_colsum(scale, x, blocks):
    parts, chunk, width = x.shape
    high = scale.astype(jnp.bfloat16)
    rest = scale - high.astype(jnp.float32)
    middle = rest.astype(jnp.bfloat16)
    low = (rest - middle.astype(jnp.float32)).astype(jnp.bfloat16)
    thirds = jnp.concatenate(
        [high[None], middle[None], low[None], jnp.zeros((13, scale.shape[0]), jnp.bfloat16)]
    )
    return pl.pallas_call(
        colsum_kernel,
        in_specs=[VMEM, ANY],
        out_specs=VMEM,
        out_shape=jax.ShapeDtypeStruct((blocks, width // blocks), jnp.float32),
        scratch_shapes=[pltpu.VMEM(x.shape, jnp.bfloat16), pltpu.SemaphoreType.DMA((4,))],
        compiler_params=pltpu.CompilerParams(vmem_limit_bytes=40 << 20),
        cost_estimate=cost(2 * 16 * parts * chunk * width, 4 << 20),
        name="weighted_colsum",
    )(thirds, pltpu.with_memory_space_constraint(x, pltpu.HBM))


def final_kernel(lines, x_ref, first_ref, second_ref, o_ref):
    step = pl.program_id(0)
    rows, slots, half = o_ref.shape
    chunk = x_ref.shape[2]
    for part in range(rows // chunk):
        at = step * (rows // chunk) + part
        first = first_ref[pl.ds(pl.multiple_of(at * chunk, chunk), chunk), :]
        first = jnp.broadcast_to(first, (chunk, half))
        values = [
            x_ref[at, slot].astype(jnp.float32) * first * second_ref[pl.ds(lines[slot], 1), :]
            for slot in range(slots)
        ]
        o_ref[part * chunk : (part + 1) * chunk] = jnp.concatenate(
            [value.astype(jnp.bfloat16) for value in values], axis=1
        ).reshape(chunk, slots, half)


def final_scale(lines, x, first, second, parts):
    col_count, slots, chunk, half = x.shape
    steps = col_count // parts
    return pl.pallas_call(
        final_kernel,
        grid_spec=pltpu.PrefetchScalarGridSpec(
            num_scalar_prefetch=1,
            grid=(steps,),
            in_specs=[VMEM, VMEM, VMEM],
            out_specs=pl.BlockSpec((parts * chunk, slots, half), lambda i, n: (i, 0, 0)),
        ),
        out_shape=pltpu.HBM((col_count * chunk, slots, half), jnp.bfloat16),
        compiler_params=params(),
        cost_estimate=cost(0, 5 << 20),
        name="final_scale",
    )(lines, x, first, second)


def swap(value, axis, bit):
    size = lax.axis_size(axis)
    return lax.ppermute(value, axis, [(i, i ^ bit) for i in range(size)])


def move(value, by, bits):
    rows, cols, cores = (lax.axis_size(axis) for axis in ("row", "col", "pan"))
    pairs = [
        ((r * cols + c) * cores + h, ((r + by) % rows * cols + (c ^ bits[h])) * cores + h)
        for r in range(rows)
        for c in range(cols)
        for h in range(cores)
    ]
    return lax.ppermute(value, ("row", "col", "pan"), pairs)


def four(value, low, by):
    return [value] + [move(value, by, (k * low, k * low)) for k in (1, 2, 3)]


def shared_pairs(value, low, by):
    return move(value, by, (0, low)), move(value, by, (2 * low, 3 * low))


def shared_sum(value, low, by):
    first, second = shared_pairs(value, low, by)
    both = first + second
    return both + swap(both, "pan", 1)


def local(
    plan_values,
    plan_blocks,
    first_values,
    first_blocks,
    second_values,
    second_blocks,
    weight_first,
    weight_second,
    offset_first,
    offset_second,
):
    col_count = lax.axis_size("col")
    column = lax.axis_index("col")
    side = lax.axis_index("pan")
    blocks_here = second_blocks.shape[0]
    panel_rows, slots, half = plan_values.shape
    block_size = first_values.shape[2]
    chunk = panel_rows // col_count
    plan_width = float(slots * col_count * block_size)

    named = plan_blocks[0]
    product = first_product(
        plan_values, first_values, first_blocks, named, side.reshape(1), col_count
    )
    arrived = lax.all_to_all(product, "col", split_axis=0, concat_axis=0, tiled=True)
    merged, ids = merge(arrived, col_count, blocks_here, chunk)
    merged, offset_first, offset_second = lax.optimization_barrier(
        (merged, offset_first, offset_second)
    )
    mine = lax.all_to_all(merged, "col", split_axis=0, concat_axis=0, tiled=True)
    ids = ids[:, :slots].reshape(-1)
    own_blocks = column * blocks_here + jnp.arange(blocks_here)
    present = jnp.any(ids[:, None] == own_blocks[None, :], axis=0)
    other = swap(mine, "pan", 1)
    near, matrix_other = second_near(mine, second_values, second_blocks, side.reshape(1))
    offsets = jnp.where(present[:, None], offset_second, jnp.inf).reshape(1, -1)
    kernel, totals = second_far(other, matrix_other, near, offset_first[:, None], offsets, 8)
    back = lax.all_to_all(kernel, "col", split_axis=0, concat_axis=0, tiled=True)

    totals = totals.reshape(blocks_here, -1)
    totals = totals + swap(totals, "pan", 1)
    totals = shared_sum(totals, 1, 1)
    totals = shared_sum(totals, 4, -1)
    scale_first = weight_first * plan_width / totals.reshape(-1)
    colsum = weighted_colsum(scale_first, kernel, blocks_here)
    sums = jnp.concatenate(
        [colsum, jnp.broadcast_to(present.astype(jnp.float32)[:, None], colsum.shape)]
    )
    sums = sums + swap(sums, "row", 1)
    sums = sums + swap(sums, "row", 2)
    ids, sums = lax.optimization_barrier((ids, sums))
    sums = sums + swap(sums, "row", 7)
    colsum = sums[:blocks_here]
    counts = sums[blocks_here:, :1] * float(panel_rows)
    scale_second = weight_second * counts / jnp.where(counts > 0, colsum, 1.0)
    all_second = jnp.concatenate(four(scale_second, 1, 1))
    all_second = jnp.concatenate(four(all_second, 4, 1))
    lines = ((named // blocks_here) ^ column) * blocks_here + named % blocks_here

    chosen = select(ids, back, slots, half)
    home = lax.all_to_all(chosen, "col", split_axis=0, concat_axis=0, tiled=True)
    new_plan = final_scale(lines, home, scale_first[:, None], all_second, 8)
    return (new_plan, scale_first, scale_second)


def solution(mesh):
    return jax.shard_map(
        local,
        mesh=mesh,
        in_specs=(
            P("row", "col", "pan"),
            P("row", "col"),
            P("row", None, None, None),
            P("row", None),
            P("col", None, None, "pan"),
            P("col", None),
            P("row"),
            P("col", "pan"),
            P("row"),
            P("col", "pan"),
        ),
        out_specs=(P("row", "col", "pan"), P("row"), P("col", "pan")),
        check_vma=False,
    )
```

```python
import functools
import jax
import jax.numpy as jnp
from jax import lax
from jax.experimental import pallas as pl
from jax.experimental.pallas import tpu as pltpu
from jax.sharding import PartitionSpec as P

LARGEST = float(jnp.finfo(jnp.bfloat16).max)


def params(mebibytes=40):
    return pltpu.CompilerParams(
        dimension_semantics=("arbitrary",), vmem_limit_bytes=mebibytes << 20
    )


def cost(flops, moved):
    return pl.CostEstimate(flops=flops, bytes_accessed=moved, transcendentals=0)


VMEM = pl.BlockSpec(memory_space=pltpu.VMEM)
SMEM = pl.BlockSpec(memory_space=pltpu.SMEM)
ANY = pl.BlockSpec(memory_space=pl.ANY)


def first_kernel(place, near, named, x_hbm, c_hbm, o_hbm, x, c, flat, out, x_sem, c_sem, o_sem):
    tiles, count, rows, _ = c.shape
    slots, half = x.shape[1:]
    chunk = x.shape[0] // out.shape[0]
    parts = rows // chunk

    def load_x(tile):
        part = pl.ds(tile * rows, rows)
        return pltpu.make_async_copy(x_hbm.at[part], x.at[part], x_sem.at[tile])

    def load_c(tile):
        return pltpu.make_async_copy(c_hbm.at[tile], c.at[tile], c_sem.at[tile])

    def store(tile):
        part = pl.ds(tile * parts, parts)
        return pltpu.make_async_copy(out.at[part], o_hbm.at[part], o_sem.at[tile])

    for tile in range(tiles):
        load_x(tile).start()
    for tile in range(tiles):
        load_c(tile).start()
    lanes = lax.broadcasted_iota(jnp.int32, (8, half), 1)
    line = jnp.zeros((8, half), jnp.int32)
    for slot in range(slots):
        line = jnp.where(lanes == slot, named[slot], line)
    for part in range(out.shape[0]):
        out[part, slots * chunk :] = line.astype(jnp.float32).astype(jnp.bfloat16)
    for tile in range(tiles):
        load_x(tile).wait()
        flat[tile] = x[tile * rows : (tile + 1) * rows].reshape(rows, slots * half)
    for tile in range(tiles):
        load_c(tile).wait()
        total = None
        for q in range(count):
            term = jnp.dot(c[tile, q], flat[near[tile, q]], preferred_element_type=jnp.float32)
            total = term if total is None else total + term
        total = total.astype(jnp.bfloat16)
        for part in range(parts):
            for slot in range(slots):
                out[tile * parts + part, slot * chunk : (slot + 1) * chunk] = total[
                    part * chunk : (part + 1) * chunk, slot * half : (slot + 1) * half
                ]
        store(tile).start()
    for tile in range(tiles):
        store(tile).wait()

    @pl.when(place[0] == 1)
    def _():
        pl.delay(14000)


def first_product(x, values, near, named, place, col_count):
    panel_rows, slots, half = x.shape
    tiles, count, rows, _ = values.shape
    chunk = panel_rows // col_count
    shape = (col_count, slots * chunk + 8, half)
    return pl.pallas_call(
        first_kernel,
        in_specs=[SMEM, SMEM, SMEM, ANY, ANY],
        out_specs=ANY,
        out_shape=pltpu.HBM(shape, jnp.bfloat16),
        scratch_shapes=[
            pltpu.VMEM(x.shape, jnp.bfloat16),
            pltpu.VMEM(values.shape, jnp.bfloat16),
            pltpu.VMEM((tiles, rows, slots * half), jnp.bfloat16),
            pltpu.VMEM(shape, jnp.bfloat16),
            pltpu.SemaphoreType.DMA((tiles,)),
            pltpu.SemaphoreType.DMA((tiles,)),
            pltpu.SemaphoreType.DMA((tiles,)),
        ],
        compiler_params=pltpu.CompilerParams(vmem_limit_bytes=60 << 20),
        cost_estimate=cost(2 * panel_rows * count * rows * slots * half, 6 << 20),
        name="first_product",
    )(place, near, named, x, values)


def merge_kernel(x_ref, o_ref, ids_ref, total, ids, sem):
    sources, height, half = x_ref.shape
    _, chunk, width = o_ref.shape
    slots = (height - 8) // chunk
    ids_ref[...] = x_ref[:, height - 8 :].astype(jnp.float32)[:, 0].astype(jnp.int32)
    copy = pltpu.make_async_copy(ids_ref, ids, sem)
    copy.start()
    total[...] = jnp.zeros_like(total)
    copy.wait()
    for source in range(sources):
        for slot in range(slots):
            piece = x_ref[source, slot * chunk : (slot + 1) * chunk]
            total[ids[source, slot]] += piece.astype(jnp.float32)
    blocks = width // half
    for panel in range(o_ref.shape[0]):
        for block in range(blocks):
            o_ref[panel, :, block * half : (block + 1) * half] = total[
                panel * blocks + block
            ].astype(jnp.bfloat16)


def merge(x, panels, blocks, chunk):
    sources, _, half = x.shape
    return pl.pallas_call(
        merge_kernel,
        in_specs=[VMEM],
        out_specs=[VMEM, VMEM],
        out_shape=[
            jax.ShapeDtypeStruct((panels, chunk, blocks * half), jnp.bfloat16),
            jax.ShapeDtypeStruct((sources, half), jnp.int32),
        ],
        scratch_shapes=[
            pltpu.VMEM((panels * blocks, chunk, half), jnp.float32),
            pltpu.SMEM((sources, half), jnp.int32),
            pltpu.SemaphoreType.DMA,
        ],
        compiler_params=pltpu.CompilerParams(vmem_limit_bytes=40 << 20),
        cost_estimate=cost(0, 8 << 20),
        name="merge",
    )(x)


def select_kernel(ids, x_ref, o_hbm, out, sem):
    sources, slots, chunk, half = out.shape
    blocks = x_ref.shape[2] // half
    groups = sem.shape[0]
    size = sources // groups

    def store(group):
        part = pl.ds(group * size, size)
        return pltpu.make_async_copy(out.at[part], o_hbm.at[part], sem.at[group])

    for group in range(groups):
        for source in range(group * size, (group + 1) * size):
            for slot in range(slots):
                block = ids[source * slots + slot]
                lanes = pl.ds(pl.multiple_of(lax.rem(block, blocks) * half, half), half)
                out[source, slot] = x_ref[lax.div(block, blocks), :, lanes]
        store(group).start()
    for group in range(groups):
        store(group).wait()


def select(ids, x, slots, half):
    sources, chunk, _ = x.shape
    shape = (sources, slots, chunk, half)
    return pl.pallas_call(
        select_kernel,
        in_specs=[SMEM, VMEM],
        out_specs=ANY,
        out_shape=pltpu.HBM(shape, jnp.bfloat16),
        scratch_shapes=[pltpu.VMEM(shape, jnp.bfloat16), pltpu.SemaphoreType.DMA((4,))],
        compiler_params=pltpu.CompilerParams(vmem_limit_bytes=40 << 20),
        cost_estimate=cost(0, 4 << 20),
        name="select",
    )(ids, x)


def near_kernel(near, place, x_ref, v_hbm, o_ref, other_ref, v, mine_ref, sem):
    parts, chunk, depth = x_ref.shape
    blocks, count, rows, half = v.shape

    def load(block):
        return pltpu.make_async_copy(v_hbm.at[block], v.at[block], sem.at[block])

    for block in range(blocks):
        load(block).start()
    mine_ref[...] = jnp.zeros_like(mine_ref)
    other_ref[...] = jnp.zeros_like(other_ref)
    mine = pl.multiple_of(place[0] * half, half)
    other = pl.multiple_of((1 - place[0]) * half, half)
    for block in range(blocks):
        load(block).wait()
        own = slice(block * half, (block + 1) * half)
        for q in range(count):
            target = pl.ds(pl.multiple_of(near[block, q] * half, half), half)
            mine_ref[own, target] = v[block, q, pl.ds(mine, half), :]
            other_ref[own, target] = v[block, q, pl.ds(other, half), :]
    side = parts // 2
    for part in range(2):
        o_ref[part * side * chunk : (part + 1) * side * chunk] = jnp.dot(
            x_ref[part * side : (part + 1) * side].reshape(side * chunk, depth),
            mine_ref[...],
            preferred_element_type=jnp.float32,
        )


def second_near(x, values, near, place):
    parts, chunk, depth = x.shape
    blocks, count, rows, half = values.shape
    columns = blocks * half
    return pl.pallas_call(
        near_kernel,
        in_specs=[SMEM, SMEM, VMEM, ANY],
        out_specs=[VMEM, VMEM],
        out_shape=[
            jax.ShapeDtypeStruct((parts * chunk, columns), jnp.float32),
            jax.ShapeDtypeStruct((depth, columns), jnp.bfloat16),
        ],
        scratch_shapes=[
            pltpu.VMEM(values.shape, jnp.bfloat16),
            pltpu.VMEM((depth, columns), jnp.bfloat16),
            pltpu.SemaphoreType.DMA((blocks,)),
        ],
        compiler_params=pltpu.CompilerParams(vmem_limit_bytes=40 << 20),
        cost_estimate=cost(2 * parts * chunk * depth * columns, 8 << 20),
        name="second_near",
    )(near, place, x, pltpu.with_memory_space_constraint(values, pltpu.HBM))


def far_kernel(x_ref, m_ref, near_ref, first_ref, second_ref, o_ref, sum_ref):
    parts, chunk, columns = o_ref.shape
    rows, half = parts * chunk, 128
    step = pl.program_id(0)
    left = x_ref[pl.ds(step * parts, parts)].reshape(rows, x_ref.shape[2])
    own = pl.ds(pl.multiple_of(step * rows, rows), rows)
    first = jnp.broadcast_to(first_ref[own, :], (rows, half))
    partial = None
    for pair in range(0, columns, 2 * half):
        far = jnp.dot(left, m_ref[:, pair : pair + 2 * half], preferred_element_type=jnp.float32)
        for at in (0, half):
            lanes = slice(pair + at, pair + at + half)
            value = jnp.exp(
                far[:, at : at + half] + near_ref[own, lanes] - first - second_ref[:, lanes]
            )
            partial = value if partial is None else partial + value
            rounded = jnp.minimum(value, LARGEST).astype(jnp.bfloat16)
            o_ref[:, :, lanes] = rounded.reshape(parts, chunk, half)
    sum_ref[0] = jnp.sum(partial.T, axis=0, keepdims=True)


def second_far(x, matrix, near, first, second, parts):
    col_count, chunk, depth = x.shape
    rows = parts * chunk
    columns = matrix.shape[1]
    steps = col_count // parts
    return pl.pallas_call(
        far_kernel,
        grid=(steps,),
        in_specs=[VMEM] * 5,
        out_specs=[
            pl.BlockSpec((parts, chunk, columns), lambda i: (i, 0, 0)),
            pl.BlockSpec((1, 1, rows), lambda i: (i, 0, 0)),
        ],
        out_shape=[
            pltpu.HBM((col_count, chunk, columns), jnp.bfloat16),
            jax.ShapeDtypeStruct((steps, 1, rows), jnp.float32),
        ],
        compiler_params=params(),
        cost_estimate=cost(2 * col_count * chunk * depth * columns, 10 << 20),
        name="second_far",
    )(x, matrix, near, first, second)


def colsum_kernel(s_ref, x_hbm, o_ref, x, sem):
    groups = sem.shape[0]
    parts, chunk, width = x.shape
    size = parts // groups

    def load(group):
        part = pl.ds(group * size, size)
        return pltpu.make_async_copy(x_hbm.at[part], x.at[part], sem.at[group])

    for group in range(groups):
        load(group).start()
    total = None
    for group in range(groups):
        load(group).wait()
        rows = slice(group * size * chunk, (group + 1) * size * chunk)
        term = jnp.dot(
            s_ref[:, rows],
            x[group * size : (group + 1) * size].reshape(size * chunk, width),
            preferred_element_type=jnp.float32,
        )
        total = term if total is None else total + term
    blocks, half = o_ref.shape
    line = total[0:1] + total[1:2] + total[2:3]
    for block in range(blocks):
        o_ref[block : block + 1] = line[:, block * half : (block + 1) * half]


def weighted_colsum(scale, x, blocks):
    parts, chunk, width = x.shape
    high = scale.astype(jnp.bfloat16)
    rest = scale - high.astype(jnp.float32)
    middle = rest.astype(jnp.bfloat16)
    low = (rest - middle.astype(jnp.float32)).astype(jnp.bfloat16)
    thirds = jnp.concatenate(
        [high[None], middle[None], low[None], jnp.zeros((13, scale.shape[0]), jnp.bfloat16)]
    )
    return pl.pallas_call(
        colsum_kernel,
        in_specs=[VMEM, ANY],
        out_specs=VMEM,
        out_shape=jax.ShapeDtypeStruct((blocks, width // blocks), jnp.float32),
        scratch_shapes=[pltpu.VMEM(x.shape, jnp.bfloat16), pltpu.SemaphoreType.DMA((4,))],
        compiler_params=pltpu.CompilerParams(vmem_limit_bytes=40 << 20),
        cost_estimate=cost(2 * 16 * parts * chunk * width, 4 << 20),
        name="weighted_colsum",
    )(thirds, pltpu.with_memory_space_constraint(x, pltpu.HBM))


def final_kernel(lines, x_ref, first_ref, second_ref, o_ref):
    step = pl.program_id(0)
    rows, slots, half = o_ref.shape
    chunk = x_ref.shape[2]
    for part in range(rows // chunk):
        at = step * (rows // chunk) + part
        first = first_ref[pl.ds(pl.multiple_of(at * chunk, chunk), chunk), :]
        first = jnp.broadcast_to(first, (chunk, half))
        values = [
            x_ref[at, slot].astype(jnp.float32) * first * second_ref[pl.ds(lines[slot], 1), :]
            for slot in range(slots)
        ]
        o_ref[part * chunk : (part + 1) * chunk] = jnp.concatenate(
            [value.astype(jnp.bfloat16) for value in values], axis=1
        ).reshape(chunk, slots, half)


def final_scale(lines, x, first, second, parts):
    col_count, slots, chunk, half = x.shape
    steps = col_count // parts
    return pl.pallas_call(
        final_kernel,
        grid_spec=pltpu.PrefetchScalarGridSpec(
            num_scalar_prefetch=1,
            grid=(steps,),
            in_specs=[VMEM, VMEM, VMEM],
            out_specs=pl.BlockSpec((parts * chunk, slots, half), lambda i, n: (i, 0, 0)),
        ),
        out_shape=pltpu.HBM((col_count * chunk, slots, half), jnp.bfloat16),
        compiler_params=params(),
        cost_estimate=cost(0, 5 << 20),
        name="final_scale",
    )(lines, x, first, second)


def swap(value, axis, bit):
    size = lax.axis_size(axis)
    return lax.ppermute(value, axis, [(i, i ^ bit) for i in range(size)])


def move(value, by, bits):
    rows, cols, cores = (lax.axis_size(axis) for axis in ("row", "col", "pan"))
    pairs = [
        ((r * cols + c) * cores + h, ((r + by) % rows * cols + (c ^ bits[h])) * cores + h)
        for r in range(rows)
        for c in range(cols)
        for h in range(cores)
    ]
    return lax.ppermute(value, ("row", "col", "pan"), pairs)


def four(value, low, by):
    return [value] + [move(value, by, (k * low, k * low)) for k in (1, 2, 3)]


def shared_pairs(value, low, by):
    return move(value, by, (0, low)), move(value, by, (2 * low, 3 * low))


def shared_sum(value, low, by):
    first, second = shared_pairs(value, low, by)
    both = first + second
    return both + swap(both, "pan", 1)


def local(
    plan_values,
    plan_blocks,
    first_values,
    first_blocks,
    second_values,
    second_blocks,
    weight_first,
    weight_second,
    offset_first,
    offset_second,
):
    col_count = lax.axis_size("col")
    column = lax.axis_index("col")
    side = lax.axis_index("pan")
    blocks_here = second_blocks.shape[0]
    panel_rows, slots, half = plan_values.shape
    block_size = first_values.shape[2]
    chunk = panel_rows // col_count
    plan_width = float(slots * col_count * block_size)

    named = plan_blocks[0]
    product = first_product(
        plan_values, first_values, first_blocks, named, side.reshape(1), col_count
    )
    arrived = lax.all_to_all(product, "col", split_axis=0, concat_axis=0, tiled=True)
    merged, ids = merge(arrived, col_count, blocks_here, chunk)
    merged, offset_first, offset_second = lax.optimization_barrier(
        (merged, offset_first, offset_second)
    )
    mine = lax.all_to_all(merged, "col", split_axis=0, concat_axis=0, tiled=True)
    ids = ids[:, :slots].reshape(-1)
    own_blocks = column * blocks_here + jnp.arange(blocks_here)
    present = jnp.any(ids[:, None] == own_blocks[None, :], axis=0)
    other = swap(mine, "pan", 1)
    near, matrix_other = second_near(mine, second_values, second_blocks, side.reshape(1))
    offsets = jnp.where(present[:, None], offset_second, jnp.inf).reshape(1, -1)
    kernel, totals = second_far(other, matrix_other, near, offset_first[:, None], offsets, 8)
    back = lax.all_to_all(kernel, "col", split_axis=0, concat_axis=0, tiled=True)

    totals = totals.reshape(blocks_here, -1)
    totals = totals + swap(totals, "pan", 1)
    totals = shared_sum(totals, 1, 1)
    totals = shared_sum(totals, 4, -1)
    scale_first = weight_first * plan_width / totals.reshape(-1)
    colsum = weighted_colsum(scale_first, kernel, blocks_here)
    sums = jnp.concatenate(
        [colsum, jnp.broadcast_to(present.astype(jnp.float32)[:, None], colsum.shape)]
    )
    sums = sums + swap(sums, "row", 1)
    sums = sums + swap(sums, "row", 2)
    ids, sums = lax.optimization_barrier((ids, sums))
    sums = sums + swap(sums, "row", 7)
    colsum = sums[:blocks_here]
    counts = sums[blocks_here:, :1] * float(panel_rows)
    scale_second = weight_second * counts / jnp.where(counts > 0, colsum, 1.0)
    all_second = jnp.concatenate(four(scale_second, 1, 1))
    all_second = jnp.concatenate(four(all_second, 4, 1))
    lines = ((named // blocks_here) ^ column) * blocks_here + named % blocks_here

    chosen = select(ids, back, slots, half)
    home = lax.all_to_all(chosen, "col", split_axis=0, concat_axis=0, tiled=True)
    new_plan = final_scale(lines, home, scale_first[:, None], all_second, 8)
    return (new_plan, scale_first, scale_second)


def solution(mesh):
    return jax.shard_map(
        local,
        mesh=mesh,
        in_specs=(
            P("row", "col", "pan"),
            P("row", "col"),
            P("row", None, None, None),
            P("row", None),
            P("col", None, None, "pan"),
            P("col", None),
            P("row"),
            P("col", "pan"),
            P("row"),
            P("col", "pan"),
        ),
        out_specs=(P("row", "col", "pan"), P("row"), P("col", "pan")),
        check_vma=False,
    )
```
